32 devices in a mesh: order: 16 (over z, x, core), slab: 2 (over y).
Axes of the slice: x: 2, y: 2, z: 4, core: 2. Of those that a mesh axis runs over, the one named last changes fastest.
Arguments:
- direct: float32 [16, 2, 256, 1024], P('order', None, 'slab'), may hold values from -6 to 6
- adjoint: float32 [16, 2, 256, 1024], P('order', None, 'slab'), may hold values from -6 to 6
- sound: float32 [256, 1024], P('slab'), may hold values from 0.5 to 4
- transverse: float32 [1024, 1024], replicated, may hold values from -0.1875 to 0.1875
- burner_temp: float32 [16], replicated, may hold values from -4 to 4
- burner_gain: float32 [16], replicated, may hold values from -4 to 4
- flame_cells: int32 [4096], replicated, may hold values from 0 to 262143
- flame_weight: float32 [4096], replicated, may hold values from 0.5 to 4
- offsets: int32 [4], replicated, may hold values from 1 to 15
Outputs:
- image: float32 [16, 2, 256, 1024], P('order', None, 'slab')
- coupling: float32 [16, 2, 4], P('order')
The draws below stay inside these ranges and needn't reach their ends.
All inputs are finite; a program needn't handle non-finite values.
Results may differ from the reference program's by a relative error of at most 0.0003.
Values sent between devices are 32-bit elements; how exact they have to be, the bound alone decides.
No kernel may reach another device: no remote copies, remote signals or barrier semaphores. Data moves between devices by JAX's collectives and lax.ppermute only.
A program may use at most 128 MiB of HBM per device.

```python
import math
import jax
import jax.numpy as jnp
from jax import lax

AZ = 1024
FLAMES = 4096
OFFS = 4
ORDERS = 16
AX = 256


def place_ends(entries, stream_key, low, high):
    longest = entries.shape.index(max(entries.shape))
    spots = []
    for shift in (0, 1):
        where = [jax.random.randint(jax.random.fold_in(stream_key, axis), (), 0, length) for axis, length in enumerate(entries.shape)]
        where[longest] = (where[longest] + shift) % entries.shape[longest]
        spots.append(tuple(where))
    return entries.at[spots[0]].set(low).at[spots[1]].set(high)


def level_of(key, dims, shards, low, high):
    def one(dim, blocks):
        draws = jax.random.uniform(jax.random.fold_in(jax.random.fold_in(key, 6), dim), (blocks,), jnp.float32, low / len(shards), high / len(shards))
        return jnp.repeat(jnp.exp(draws), dims[dim] // blocks).reshape((-1,) + (1,) * (len(dims) - dim - 1))

    loudness = one(*shards[0])
    for cut in shards[1:]:
        loudness = loudness * one(*cut)
    return loudness


def gaussian(own_key, shape, spread, bound, shards=(), kind=jnp.bfloat16):
    gain = level_of(own_key, shape, shards, -0.22, 0.18) if shards else 1.0
    values = jax.random.normal(own_key, shape, jnp.float32) * spread * gain
    return jnp.minimum(jnp.maximum(values, -bound), bound).astype(kind)


def setup_inputs(seed: int = 0) -> dict:
    key_of = jax.random.split(jax.random.key(seed), 10)
    return {
        "direct": gaussian(key_of[0], (ORDERS, 2, AX, AZ), 1.0, 6.0, ((0, 16), (2, 2)), jnp.float32),
        "adjoint": gaussian(key_of[1], (ORDERS, 2, AX, AZ), 1.0, 6.0, ((0, 16), (2, 2)), jnp.float32),
        "sound": jnp.clip(jnp.exp(math.log(4.0) - 2.0794415 * jax.random.uniform(key_of[2], (AX, AZ), jnp.float32) ** level_of(key_of[2], (AX, AZ), ((0, 2),), -0.2, 0.2)), 0.5, 4.0),
        "transverse": gaussian(key_of[3], (AZ, AZ), AZ ** -0.5, 0.1875, (), jnp.float32),
        "burner_temp": gaussian(key_of[4], (ORDERS,), 1.0, 4.0, (), jnp.float32),
        "burner_gain": gaussian(key_of[5], (ORDERS,), 1.0, 4.0, (), jnp.float32),
        "flame_cells": place_ends(jax.random.randint(key_of[6], (FLAMES,), 0, AX * AZ), jax.random.fold_in(key_of[6], 1), 0, (AX * AZ) - 1).astype(jnp.int32),
        "flame_weight": jnp.clip(jnp.exp(jax.random.uniform(key_of[7], (FLAMES,), jnp.float32, math.log(0.5), math.log(4.0))), 0.5, 4.0),
        "offsets": place_ends(jax.random.randint(key_of[8], (OFFS,), 1, ORDERS), jax.random.fold_in(key_of[8], 1), 1, ORDERS - 1).astype(jnp.int32),
    }


def apply_padded(padded, sound_padded, angle_now, transverse):
    center = padded[:, 1:-1]
    middle = sound_padded[1:-1]
    axial = 0.5 * (middle + sound_padded[2:]) * (center - padded[:, 2:]) + 0.5 * (middle + sound_padded[:-2]) * (center - padded[:, :-2])
    across = jnp.einsum('cxz,zw->cxw', center, transverse, precision=lax.Precision.HIGHEST)
    seam_weight = 0.5 * (middle[:, -1] + middle[:, 0])
    cos_turn = jnp.cos(angle_now)
    sin_turn = jnp.sin(angle_now)
    first_re = center[0, :, 0]
    first_im = center[1, :, 0]
    last_re = center[0, :, -1]
    last_im = center[1, :, -1]
    ahead_re = cos_turn * first_re - sin_turn * first_im
    ahead_im = sin_turn * first_re + cos_turn * first_im
    behind_re = cos_turn * last_re + sin_turn * last_im
    behind_im = cos_turn * last_im - sin_turn * last_re
    last_add = jnp.stack([seam_weight * (last_re - ahead_re), seam_weight * (last_im - ahead_im)])
    first_add = jnp.stack([seam_weight * (first_re - behind_re), seam_weight * (first_im - behind_im)])
    result = axial + across
    result = result.at[:, :, -1].add(last_add)
    result = result.at[:, :, 0].add(first_add)
    return result

def fourier_pair(values, offsets, orders):
    burner = jnp.arange(orders, dtype=jnp.int32)
    turns = offsets[:, None] * burner[None, :] % orders
    angles = 2.0 * math.pi / orders * turns.astype(values.dtype)
    real_part = lax.optimization_barrier(jnp.sum(values[None, :] * jnp.cos(angles), axis=1)) / orders
    imag_part = -lax.optimization_barrier(jnp.sum(values[None, :] * jnp.sin(angles), axis=1)) / orders
    return (real_part, imag_part)

def reference(direct, adjoint, sound, transverse, burner_temp, burner_gain, flame_cells, flame_weight, offsets):
    orders = ORDERS
    flame_field = jnp.zeros((AX * AZ,), flame_weight.dtype).at[flame_cells].add(flame_weight).reshape(AX, AZ)
    temp_re, temp_im = fourier_pair(burner_temp, offsets, orders)
    gain_re, gain_im = fourier_pair(burner_gain, offsets, orders)
    sound_padded = jnp.pad(sound, ((1, 1), (0, 0)))
    order_ids = jnp.arange(orders, dtype=jnp.int32)

    def own_image(order_now):
        angle_now = 2.0 * math.pi / orders * order_now.astype(direct.dtype)
        padded = jnp.pad(direct[order_now], ((0, 0), (1, 1), (0, 0)))
        return apply_padded(padded, sound_padded, angle_now, transverse)
    base = lax.map(own_image, order_ids)
    scale = 1.0 / math.sqrt(AX * AZ)

    def collect(order_now):
        total = base[order_now]
        adj = adjoint[order_now]
        rows_re = []
        rows_im = []
        for which in range(OFFS):
            source = (order_now - offsets[which]) % orders
            helm = base[source]
            field = direct[source]
            term_re = temp_re[which] * helm[0] - temp_im[which] * helm[1] + flame_field * (gain_re[which] * field[0] - gain_im[which] * field[1])
            term_im = temp_re[which] * helm[1] + temp_im[which] * helm[0] + flame_field * (gain_re[which] * field[1] + gain_im[which] * field[0])
            total = total + jnp.stack([term_re, term_im])
            rows_re.append(jnp.sum(adj[0] * term_re + adj[1] * term_im) * scale)
            rows_im.append(jnp.sum(adj[0] * term_im - adj[1] * term_re) * scale)
        return (total, jnp.stack([jnp.stack(rows_re), jnp.stack(rows_im)]))
    image, coupling = lax.map(collect, order_ids)
    return (image, coupling)
```

```python
import functools
import math

import jax
import jax.numpy as jnp
from jax import lax
from jax.experimental import pallas as pl
from jax.experimental.pallas import tpu as pltpu
from jax.sharding import PartitionSpec as P


VMEM = pltpu.VMEM
SMEM = pltpu.SMEM
LANES = 128
LIMIT = 28 * 1024 * 1024


def params(limit=LIMIT):
    return pltpu.CompilerParams(vmem_limit_bytes=limit)


def whole_spec(space=VMEM):
    return pl.BlockSpec(memory_space=space)


def pack_kernel(half, rows, where_ref, field_ref, above_ref, below_ref, *out_refs):
    here = where_ref[0]
    mid = field_ref.shape[2] // 2
    for t in range(half):
        site = here ^ t
        start = pl.multiple_of(site * rows, rows)
        block = 0
        for part in range(2):
            for low in range(0, rows, 8):
                for side in range(2):
                    out_refs[t][block * 8 : block * 8 + 8, :] = field_ref[
                        part, pl.ds(start + low, 8), side * mid : (side + 1) * mid
                    ]
                    block += 1
        before = jnp.maximum(start - 1, 0)
        after = jnp.minimum(start + rows, half * rows - 1)
        for part in range(2):
            up = jnp.where(site == 0, above_ref[part : part + 1, :], field_ref[part, pl.ds(before, 1), :])
            down = jnp.where(
                site == half - 1, below_ref[part : part + 1, :], field_ref[part, pl.ds(after, 1), :]
            )
            for place, row in enumerate((up, down)):
                for side in range(2):
                    at = block * 8 + part * 4 + place * 2 + side
                    out_refs[t][at : at + 1, :] = row[:, side * mid : (side + 1) * mid]


def split_kernel(full_ref, high_ref, low_ref):
    full = full_ref[...]
    high = full.astype(jnp.bfloat16)
    high_ref[...] = high
    low_ref[...] = (full - high.astype(jnp.float32)).astype(jnp.bfloat16)


def flame_kernel(rows, step, where_ref, row_ref, col_ref, weight_ref, out_ref):
    width = out_ref.shape[1]
    first = where_ref[0]
    total = jnp.zeros((3 * rows, width), jnp.float32)
    for at in range(0, row_ref.shape[1], step):
        cell_row = row_ref[:, at : at + step] - first
        cell_col = col_ref[:, at : at + step]
        weight = weight_ref[:, at : at + step]
        one = weight.astype(jnp.bfloat16).astype(jnp.float32)
        two = (weight - one).astype(jnp.bfloat16).astype(jnp.float32)
        three = weight - one - two
        hit = lax.broadcasted_iota(jnp.int32, (rows, step), 0) == cell_row
        left = jnp.concatenate([jnp.where(hit, x, 0.0) for x in (one, two, three)], axis=0)
        right = jnp.where(lax.broadcasted_iota(jnp.int32, (width, step), 0) == cell_col, 1.0, 0.0)
        total += lax.dot_general(
            left.astype(jnp.bfloat16),
            right.astype(jnp.bfloat16),
            (((1,), (1,)), ((), ())),
            preferred_element_type=jnp.float32,
        )
    out_ref[...] = total[:rows] + total[rows : 2 * rows] + total[2 * rows :]


def base_kernel(count, rows, first, cos_ref, sin_ref, *refs):
    messages = refs[:count]
    sound_ref, high_ref, low_ref = refs[count : count + 3]
    out_ref, flat_ref = refs[-2:]
    width = sound_ref.shape[1]
    mid = width // 2
    stacks = 2 * rows
    for i in range(count):
        block = 0
        for part in range(2):
            for low in range(0, rows, 8):
                for side in range(2):
                    flat_ref[
                        i * stacks + part * rows + low : i * stacks + part * rows + low + 8,
                        side * mid : (side + 1) * mid,
                    ] = messages[i][block * 8 : block * 8 + 8, :]
                    block += 1
    flat = flat_ref[...]
    high = flat.astype(jnp.bfloat16)
    low_part = (flat - high.astype(jnp.float32)).astype(jnp.bfloat16)

    def dot(a, b):
        return jnp.dot(a, b, preferred_element_type=jnp.float32)

    across = dot(high, high_ref[...]) + (dot(high, low_ref[...]) + dot(low_part, high_ref[...]))
    sound = sound_ref[...]
    middle = sound[1 : rows + 1]
    weight_up = 0.5 * (middle + sound[:rows])
    weight_down = 0.5 * (middle + sound[2 : rows + 2])
    seam = 0.5 * (middle[:, width - 1 : width] + middle[:, 0:1])
    lane = lax.broadcasted_iota(jnp.int32, (rows, width), 1)
    halo_at = 8 * (2 * (rows // 8) * 2)
    for i in range(count):
        cos_turn = cos_ref[first + i]
        sin_turn = sin_ref[first + i]
        fields = []
        for part in range(2):
            fields.append(flat[i * stacks + part * rows : i * stacks + (part + 1) * rows])
        firsts = [f[:, 0:1] for f in fields]
        lasts = [f[:, width - 1 : width] for f in fields]
        ahead = (
            cos_turn * firsts[0] - sin_turn * firsts[1],
            sin_turn * firsts[0] + cos_turn * firsts[1],
        )
        behind = (
            cos_turn * lasts[0] + sin_turn * lasts[1],
            cos_turn * lasts[1] - sin_turn * lasts[0],
        )
        for part in range(2):
            field = fields[part]
            at = halo_at + part * 4
            halo = messages[i][at : at + 4, :]
            up = jnp.concatenate([halo[0:1], halo[1:2]], axis=1)
            down = jnp.concatenate([halo[2:3], halo[3:4]], axis=1)
            above = jnp.concatenate([up, field[: rows - 1]], axis=0)
            below = jnp.concatenate([field[1:], down], axis=0)
            result = weight_down * (field - below) + weight_up * (field - above)
            result = result + across[i * stacks + part * rows : i * stacks + (part + 1) * rows]
            last_add = seam * (lasts[part] - ahead[part])
            first_add = seam * (firsts[part] - behind[part])
            result = result + jnp.where(lane == width - 1, last_add, 0.0)
            result = result + jnp.where(lane == 0, first_add, 0.0)
            out_ref[i, part] = result
            out_ref[i, 2 + part] = field


def mix_kernel(half, rows, count_offs, where_ref, index_ref, coef_ref, *refs):
    site_ref = refs[0]
    adjoint_refs = refs[1 : 1 + half]
    flame_ref = refs[1 + half]
    image_refs = refs[2 + half : 2 + 2 * half]
    sums_ref = refs[2 + 2 * half]
    width = flame_ref.shape[1]
    here = where_ref[0]

    def fold(x):
        out = x[0:8]
        for low in range(8, rows, 8):
            out = out + x[low : low + 8]
        return out

    for t in range(half):
        sources = [index_ref[t * count_offs + j] for j in range(count_offs)]
        sums = [None] * (2 * count_offs)
        for at in range(0, width, LANES):
            cut = slice(at, at + LANES)
            flame = flame_ref[:, cut]
            total_re = site_ref[t, 0, :, cut]
            total_im = site_ref[t, 1, :, cut]
            adj_re = adjoint_refs[t][0, :, cut]
            adj_im = adjoint_refs[t][1, :, cut]
            for j in range(count_offs):
                base_re = site_ref[sources[j], 0, :, cut]
                base_im = site_ref[sources[j], 1, :, cut]
                field_re = site_ref[sources[j], 2, :, cut]
                field_im = site_ref[sources[j], 3, :, cut]
                temp_re, temp_im = coef_ref[4 * j], coef_ref[4 * j + 1]
                gain_re, gain_im = coef_ref[4 * j + 2], coef_ref[4 * j + 3]
                term_re = temp_re * base_re - temp_im * base_im + flame * (gain_re * field_re - gain_im * field_im)
                term_im = temp_re * base_im + temp_im * base_re + flame * (gain_re * field_im + gain_im * field_re)
                total_re = total_re + term_re
                total_im = total_im + term_im
                add_re = fold(adj_re * term_re + adj_im * term_im)
                add_im = fold(adj_re * term_im - adj_im * term_re)
                sums[j] = add_re if sums[j] is None else sums[j] + add_re
                k = count_offs + j
                sums[k] = add_im if sums[k] is None else sums[k] + add_im
            image_refs[t][0, :, cut] = total_re
            image_refs[t][1, :, cut] = total_im
        place = pl.multiple_of((here ^ t) * 8, 8)
        rows_out = [jnp.sum(s, axis=0, keepdims=True) for s in sums]
        rows_out += [jnp.zeros((1, LANES), jnp.float32)] * (8 - len(rows_out))
        sums_ref[pl.ds(place, 8), :] = jnp.concatenate(rows_out, axis=0)


def fourier_pair(values, offsets, orders):
    burner = jnp.arange(orders, dtype=jnp.int32)
    turns = offsets[:, None] * burner[None, :] % orders
    angles = 2.0 * math.pi / orders * turns.astype(values.dtype)
    real_part = jnp.sum(values[None, :] * jnp.cos(angles), axis=1) / orders
    imag_part = -jnp.sum(values[None, :] * jnp.sin(angles), axis=1) / orders
    return (real_part, imag_part)


def local(
    direct, adjoint, sound, transverse, burner_temp, burner_gain, flame_cells, flame_weight, offsets
):
    f32 = jnp.float32
    orders = lax.axis_size("order")
    slabs = lax.axis_size("slab")
    order_now = lax.axis_index("order")
    slab_now = lax.axis_index("slab")
    half = orders // 2
    layers, width = direct.shape[2:]
    rows = layers // half
    count_offs = offsets.shape[0]
    here = order_now % half
    block_rows = 2 * (rows // 8) * 2 * 8 + 8

    def swap(value, t):
        return lax.ppermute(value, "order", [(i, i ^ t) for i in range(orders)])

    field = direct[0]
    edges = jnp.concatenate([field, sound[None]], axis=0)
    above = lax.ppermute(edges[:, layers - 1], "slab", [(i, i + 1) for i in range(slabs - 1)])
    below = lax.ppermute(edges[:, 0], "slab", [(i + 1, i) for i in range(slabs - 1)])

    where = jnp.stack([here, slab_now * layers + here * rows]).astype(jnp.int32)
    message = jax.ShapeDtypeStruct((block_rows, width // 2), f32)
    sent = pl.pallas_call(
        functools.partial(pack_kernel, half, rows),
        out_shape=[message] * half,
        in_specs=[whole_spec(SMEM)] + [whole_spec()] * 3,
        out_specs=[whole_spec()] * half,
        compiler_params=params(),
        name="pack",
    )(where[:1], field, above[:2], below[:2])

    own = [sent[0]] + [swap(sent[t], t) for t in range(1, half)]
    other = [swap(piece, half) for piece in own]

    adjoint_cut = adjoint[0].reshape(2, half, rows, width)
    adj_sent = [lax.dynamic_index_in_dim(adjoint_cut, here ^ t, 1, keepdims=False) for t in range(half)]
    adj = [adj_sent[0]] + [swap(adj_sent[t], t) for t in range(1, half)]

    high, low = pl.pallas_call(
        split_kernel,
        out_shape=[jax.ShapeDtypeStruct(transverse.shape, jnp.bfloat16)] * 2,
        in_specs=[whole_spec()],
        out_specs=[whole_spec()] * 2,
        compiler_params=params(),
        name="split",
    )(transverse)

    cells = flame_cells.reshape(1, -1)
    flame = pl.pallas_call(
        functools.partial(flame_kernel, rows, 512),
        out_shape=jax.ShapeDtypeStruct((rows, width), f32),
        in_specs=[whole_spec(SMEM)] + [whole_spec()] * 3,
        out_specs=whole_spec(),
        compiler_params=params(),
        name="flame",
    )(where[1:], cells // width, cells % width, flame_weight.reshape(1, -1))

    sound_padded = jnp.concatenate([above[2:3], sound, below[2:3]], axis=0)
    sound_site = lax.dynamic_slice_in_dim(sound_padded, here * rows, rows + 2, axis=0)

    ids = jnp.arange(orders, dtype=jnp.int32)
    angles = 2.0 * math.pi / orders * (ids ^ order_now).astype(f32)
    cos_turn, sin_turn = jnp.cos(angles), jnp.sin(angles)

    site_shape = jax.ShapeDtypeStruct((orders, 4, rows, width), f32)

    def base(pieces, first, before):
        specs = [whole_spec(SMEM)] * 2 + [whole_spec()] * (half + 3)
        args = [cos_turn, sin_turn, *pieces, sound_site, high, low]
        aliases = {}
        if before is not None:
            specs.append(pl.BlockSpec(memory_space=pl.ANY))
            args.append(before)
            aliases = {len(args) - 1: 0}
        return pl.pallas_call(
            functools.partial(base_kernel, half, rows, first),
            grid=(1,),
            out_shape=site_shape,
            in_specs=specs,
            out_specs=pl.BlockSpec((half, 4, rows, width), lambda i: (first // half, 0, 0, 0)),
            scratch_shapes=[pltpu.VMEM((half * 2 * rows, width), f32)],
            input_output_aliases=aliases,
            compiler_params=params(),
            name=f"base{first // half}",
        )(*args)

    site = base(own, 0, None)
    site = base(other, half, site)

    temp_re, temp_im = fourier_pair(burner_temp, offsets, orders)
    gain_re, gain_im = fourier_pair(burner_gain, offsets, orders)
    coef = jnp.stack([temp_re, temp_im, gain_re, gain_im], axis=1).reshape(-1)
    targets = ids[:half] ^ order_now
    index = (((targets[:, None] - offsets[None, :]) % orders) ^ order_now).reshape(-1).astype(jnp.int32)

    piece = jax.ShapeDtypeStruct((2, rows, width), f32)
    results = pl.pallas_call(
        functools.partial(mix_kernel, half, rows, count_offs),
        out_shape=[piece] * half + [jax.ShapeDtypeStruct((half * 8, LANES), f32)],
        in_specs=[whole_spec(SMEM)] * 3 + [whole_spec()] * (half + 2),
        out_specs=[whole_spec()] * (half + 1),
        compiler_params=params(),
        name="mix",
    )(where[:1], index, coef, site, *adj, flame)
    images, sums = results[:half], results[half]

    back = [images[0]] + [swap(images[t], t) for t in range(1, half)]
    groups = [list(range(half)), list(range(half, orders))]
    parts = lax.all_to_all(
        sums.reshape(half, 8, LANES), "order", 0, 0, axis_index_groups=groups, tiled=True
    )
    partial = jnp.sum(parts, axis=(0, 2))[: 2 * count_offs].reshape(2, count_offs)
    whole_sums = lax.psum(partial, "slab")
    image = jnp.zeros((2, layers, width), f32)
    for t in range(half):
        image = lax.dynamic_update_slice(image, back[t], (0, (here ^ t) * rows, 0))
    scale = 1.0 / math.sqrt(layers * slabs * width)
    return (image[None], (whole_sums * scale)[None])


def solution(mesh):
    in_specs = (
        P("order", None, "slab", None),
        P("order", None, "slab", None),
        P("slab", None),
        P(),
        P(),
        P(),
        P(),
        P(),
        P(),
    )
    out_specs = (P("order", None, "slab", None), P("order", None, None))
    return jax.shard_map(local, mesh=mesh, in_specs=in_specs, out_specs=out_specs, check_vma=False)
```

```python
import functools
import math

import jax
import jax.numpy as jnp
from jax import lax
from jax.experimental import pallas as pl
from jax.experimental.pallas import tpu as pltpu
from jax.sharding import PartitionSpec as P


VMEM = pltpu.VMEM
SMEM = pltpu.SMEM
LANES = 128
LATE = 2
BARE = 2
LAST = 2
LIMIT = 20 * 1024 * 1024


def first_kernel(half, rows, partners, direct_ref, sound_ref, *refs):
    body_refs = refs[: len(partners)]
    top_ref, bottom_ref, *block_refs, sems = refs[len(partners) :]
    layers, width = sound_ref.shape
    mid = width // 2
    here = lax.axis_index("order") % half
    copies = []

    def begin(source, target):
        copies.append(pltpu.make_async_copy(source, target, sems.at[len(copies)]))
        copies[-1].start()

    for i, low in enumerate((0, layers - 8)):
        begin(direct_ref.at[:, pl.ds(low, 8), :], block_refs[2 * i])
        begin(sound_ref.at[pl.ds(low, 8), :], block_refs[2 * i + 1])
    for t, body_ref in zip(partners, body_refs):
        start = pl.multiple_of((here ^ t) * rows, rows)
        begin(direct_ref.at[:, pl.ds(start, rows), :], body_ref)
    for copy in copies[:4]:
        copy.wait()
    for i, (out_ref, row) in enumerate(((top_ref, 0), (bottom_ref, 7))):
        for part in range(2):
            for side in range(2):
                out_ref[2 * part + side, :] = block_refs[2 * i][part, row, side * mid : (side + 1) * mid]
        for side in range(2):
            out_ref[4 + side, :] = block_refs[2 * i + 1][row, side * mid : (side + 1) * mid]
            out_ref[6 + side, :] = jnp.zeros((mid,), jnp.float32)
    if lax.axis_size("slab") == 2:
        top_ref[...] = jnp.where(lax.axis_index("slab") == 0, bottom_ref[...], top_ref[...])
    for copy in copies[4:]:
        copy.wait()


def pack_kernel(half, rows, bare, field_ref, sound_ref, above_ref, below_ref, *out_refs):
    here = lax.axis_index("order") % half
    slab = lax.axis_index("slab")
    has_above, has_below = slab > 0, slab < lax.axis_size("slab") - 1
    width = field_ref.shape[2]
    mid = width // 2
    for t in range(half):
        site = here ^ t
        start = pl.multiple_of(site * rows, rows)
        block = 0
        for part in range(2):
            for low in range(0, rows, 8):
                for side in range(2):
                    out_refs[t][block * 8 : block * 8 + 8, :] = field_ref[
                        part, pl.ds(start + low, 8), side * mid : (side + 1) * mid
                    ]
                    block += 1
        before = jnp.maximum(start - 1, 0)
        after = jnp.minimum(start + rows, half * rows - 1)
        for part in range(2):
            for side in range(2):
                cut = slice(side * mid, (side + 1) * mid)
                from_slab = 2 * part + side
                edge = jnp.where(has_above, above_ref[from_slab : from_slab + 1, :], 0.0)
                up = jnp.where(site == 0, edge, field_ref[part, pl.ds(before, 1), cut])
                edge = jnp.where(has_below, below_ref[from_slab : from_slab + 1, :], 0.0)
                down = jnp.where(site == half - 1, edge, field_ref[part, pl.ds(after, 1), cut])
                for place, value in enumerate((up, down)):
                    at = part * 4 + place * 2 + side
                    out_refs[t][block * 8 + at : block * 8 + at + 1, :] = value
                    if t in bare:
                        out_refs[half + bare.index(t)][at : at + 1, :] = value
    site_ref = out_refs[half + len(bare)]
    start = pl.multiple_of(here * rows, rows)
    site_ref[0:rows, :] = sound_ref[pl.ds(start, rows), :]
    before = jnp.maximum(start - 1, 0)
    after = jnp.minimum(start + rows, half * rows - 1)
    for side in range(2):
        cut = slice(side * mid, (side + 1) * mid)
        edge = jnp.where(has_above, above_ref[4 + side : 5 + side, :], 0.0)
        site_ref[rows : rows + 1, cut] = jnp.where(here == 0, edge, sound_ref[pl.ds(before, 1), cut])
        edge = jnp.where(has_below, below_ref[4 + side : 5 + side, :], 0.0)
        site_ref[rows + 1 : rows + 2, cut] = jnp.where(here == half - 1, edge, sound_ref[pl.ds(after, 1), cut])


def table_kernel(orders, offsets_ref, temp_ref, gain_ref, turn_ref, coef_ref):
    step = 2.0 * math.pi / orders
    own = lax.axis_index("order")
    ids = lax.broadcasted_iota(jnp.int32, (orders, LANES), 0) ^ own
    angles = step * ids.astype(jnp.float32)
    turn_ref[0:orders, :] = jnp.cos(angles)
    turn_ref[orders:, :] = jnp.sin(angles)
    row = lax.broadcasted_iota(jnp.int32, (8, orders), 0)
    offset = jnp.zeros((8, orders), jnp.int32)
    for j in range(offsets_ref.shape[0]):
        offset = jnp.where(row == j, offsets_ref[j], offset)
    turns = (offset * lax.broadcasted_iota(jnp.int32, (8, orders), 1)) & (orders - 1)
    angles = step * turns.astype(jnp.float32)
    cos, sin = jnp.cos(angles), jnp.sin(angles)
    for p, (values_ref, wave, sign) in enumerate(
        ((temp_ref, cos, 1.0), (temp_ref, sin, -1.0), (gain_ref, cos, 1.0), (gain_ref, sin, -1.0))
    ):
        total = sign * jnp.sum(values_ref[...] * wave, axis=1, keepdims=True) / orders
        coef_ref[8 * p : 8 * p + 8, :] = jnp.broadcast_to(total, (8, LANES))


def split_kernel(full_ref, high_ref, low_ref):
    full = full_ref[...]
    high = full.astype(jnp.bfloat16)
    high_ref[...] = high
    low_ref[...] = (full - high.astype(jnp.float32)).astype(jnp.bfloat16)


def flame_kernel(half, rows, step, cells_ref, weight_ref, out_ref):
    width = out_ref.shape[1]
    shift = width.bit_length() - 1
    first = lax.axis_index("slab") * (half * rows) + lax.axis_index("order") % half * rows
    total = jnp.zeros((3 * rows, width), jnp.float32)
    for at in range(0, cells_ref.shape[0], step):
        cells = jnp.concatenate([cells_ref[i : i + 1, :] for i in range(at, at + step)], axis=1)
        weight = jnp.concatenate([weight_ref[i : i + 1, :] for i in range(at, at + step)], axis=1)
        cell_row = (cells >> shift) - first
        cell_col = cells & (width - 1)
        one = weight.astype(jnp.bfloat16).astype(jnp.float32)
        two = (weight - one).astype(jnp.bfloat16).astype(jnp.float32)
        three = weight - one - two
        hit = lax.broadcasted_iota(jnp.int32, (rows, step * LANES), 0) == cell_row
        left = jnp.concatenate([jnp.where(hit, x, 0.0) for x in (one, two, three)], axis=0)
        right = jnp.where(lax.broadcasted_iota(jnp.int32, (width, step * LANES), 0) == cell_col, 1.0, 0.0)
        total += lax.dot_general(
            left.astype(jnp.bfloat16),
            right.astype(jnp.bfloat16),
            (((1,), (1,)), ((), ())),
            preferred_element_type=jnp.float32,
        )
    out_ref[...] = total[:rows] + total[rows : 2 * rows] + total[2 * rows :]


def fill_flat(pieces, rows, flat_ref):
    mid = flat_ref.shape[1] // 2
    for i, (body_ref, _) in enumerate(pieces):
        first = i * 2 * rows
        if len(body_ref.shape) == 3:
            flat_ref[first : first + rows, :] = body_ref[0]
            flat_ref[first + rows : first + 2 * rows, :] = body_ref[1]
            continue
        block = 0
        for low in range(0, 2 * rows, 8):
            for side in range(2):
                flat_ref[first + low : first + low + 8, side * mid : (side + 1) * mid] = body_ref[
                    block * 8 : block * 8 + 8, :
                ]
                block += 1


def operate(pieces, rows, places, turn_ref, sound_ref, high_ref, low_ref, flat_ref, out_ref):
    width = sound_ref.shape[1]
    stacks = 2 * rows
    fill_flat(pieces, rows, flat_ref)
    flat = flat_ref[...]
    high = flat.astype(jnp.bfloat16)
    low_part = (flat - high.astype(jnp.float32)).astype(jnp.bfloat16)

    def dot(a, b):
        return jnp.dot(a, b, preferred_element_type=jnp.float32)

    across = dot(high, high_ref[...]) + (dot(high, low_ref[...]) + dot(low_part, high_ref[...]))
    orders = turn_ref.shape[0] // 2
    middle = sound_ref[0:rows, :]
    sound_up = jnp.concatenate([sound_ref[rows : rows + 1, :], middle[: rows - 1]], axis=0)
    sound_down = jnp.concatenate([middle[1:], sound_ref[rows + 1 : rows + 2, :]], axis=0)
    weight_up = 0.5 * (middle + sound_up)
    weight_down = 0.5 * (middle + sound_down)
    seam = 0.5 * (middle[:, width - 1 : width] + middle[:, 0:1])
    lane = lax.broadcasted_iota(jnp.int32, (rows, width), 1)
    for i, (_, halo_ref) in enumerate(pieces):
        at = places[i]
        cos_turn = turn_ref[at : at + 1, 0:1]
        sin_turn = turn_ref[orders + at : orders + at + 1, 0:1]
        fields = []
        for part in range(2):
            fields.append(flat[i * stacks + part * rows : i * stacks + (part + 1) * rows])
        firsts = [f[:, 0:1] for f in fields]
        lasts = [f[:, width - 1 : width] for f in fields]
        ahead = (
            cos_turn * firsts[0] - sin_turn * firsts[1],
            sin_turn * firsts[0] + cos_turn * firsts[1],
        )
        behind = (
            cos_turn * lasts[0] + sin_turn * lasts[1],
            cos_turn * lasts[1] - sin_turn * lasts[0],
        )
        halo_rows = halo_ref[halo_ref.shape[0] - 8 :, :]
        for part in range(2):
            field = fields[part]
            halo = halo_rows[part * 4 : part * 4 + 4]
            up = jnp.concatenate([halo[0:1], halo[1:2]], axis=1)
            down = jnp.concatenate([halo[2:3], halo[3:4]], axis=1)
            above = jnp.concatenate([up, field[: rows - 1]], axis=0)
            below = jnp.concatenate([field[1:], down], axis=0)
            result = weight_down * (field - below) + weight_up * (field - above)
            result = result + across[i * stacks + part * rows : i * stacks + (part + 1) * rows]
            last_add = seam * (lasts[part] - ahead[part])
            first_add = seam * (firsts[part] - behind[part])
            result = result + jnp.where(lane == width - 1, last_add, 0.0)
            result = result + jnp.where(lane == 0, first_add, 0.0)
            out_ref[i, part] = result
            out_ref[i, 2 + part] = field


def pair_up(refs, split):
    apart = [(refs[2 * i], refs[2 * i + 1]) for i in range(split)]
    return apart + [(r, r) for r in refs[2 * split :]]


def base_kernel(count, rows, places, split, turn_ref, *refs):
    taken = count + split
    pieces = pair_up(refs[:taken], split)
    sound_ref, high_ref, low_ref = refs[taken : taken + 3]
    out_ref, flat_ref = refs[-2:]
    operate(pieces, rows, places, turn_ref, sound_ref, high_ref, low_ref, flat_ref, out_ref)


def add_terms(coefs, source_ref, source, flame_ref, image_ref):
    temp_re, temp_im, gain_re, gain_im = coefs
    for at in range(0, flame_ref.shape[1], LANES):
        cut = slice(at, at + LANES)
        flame = flame_ref[:, cut]
        base_re = source_ref[source, 0, :, cut]
        base_im = source_ref[source, 1, :, cut]
        field_re = source_ref[source, 2, :, cut]
        field_im = source_ref[source, 3, :, cut]
        image_ref[0, :, cut] += (
            temp_re * base_re - temp_im * base_im + flame * (gain_re * field_re - gain_im * field_im)
        )
        image_ref[1, :, cut] += (
            temp_re * base_im + temp_im * base_re + flame * (gain_re * field_im + gain_im * field_re)
        )


def inner_products(rows, coefs, source_ref, source, adjoint_ref, flame_ref, sums_ref, at_re, at_im):
    temp_re, temp_im, gain_re, gain_im = coefs

    def fold(x):
        out = x[0:8]
        for low in range(8, rows, 8):
            out = out + x[low : low + 8]
        return out

    sums = [jnp.zeros((8, LANES), jnp.float32)] * 4
    for at in range(0, flame_ref.shape[1], LANES):
        cut = slice(at, at + LANES)
        flame = flame_ref[:, cut]
        adj_re = adjoint_ref[0, :, cut]
        adj_im = adjoint_ref[1, :, cut]
        base_re = source_ref[source, 0, :, cut]
        base_im = source_ref[source, 1, :, cut]
        field_re = flame * source_ref[source, 2, :, cut]
        field_im = flame * source_ref[source, 3, :, cut]
        sums[0] = sums[0] + fold(adj_re * base_re + adj_im * base_im)
        sums[1] = sums[1] + fold(adj_re * base_im - adj_im * base_re)
        sums[2] = sums[2] + fold(adj_re * field_re + adj_im * field_im)
        sums[3] = sums[3] + fold(adj_re * field_im - adj_im * field_re)
    sums_ref[at_re] = temp_re * sums[0] - temp_im * sums[1] + gain_re * sums[2] - gain_im * sums[3]
    sums_ref[at_im] = temp_re * sums[1] + temp_im * sums[0] + gain_re * sums[3] + gain_im * sums[2]


def coefs_of(coef_ref, j):
    return tuple(coef_ref[8 * p + j : 8 * p + j + 1, :] for p in range(4))


def source_of(half, offsets_ref, t, j):
    own = lax.axis_index("order")
    orders = 2 * half
    place = (((own ^ t) - offsets_ref[j] + orders) & (orders - 1)) ^ own
    quarter = half // 2
    later = half + (place & (quarter - 1)) * 2 + ((place & quarter) // quarter)
    return jnp.where(place < half, place, later)


def cross_order(half):
    return [t + far for t in range(half // 2) for far in (0, half // 2)]


def early_kernel(half, count_offs, ready, offsets_ref, coef_ref, own_ref, cross_ref, flame_ref, image_ref):
    for t in range(half):
        image_ref[t, 0] = own_ref[t, 0]
        image_ref[t, 1] = own_ref[t, 1]
        for j in range(count_offs):
            source = source_of(half, offsets_ref, t, j)

            @pl.when(source < half)
            def _(t=t, j=j, source=source):
                add_terms(coefs_of(coef_ref, j), own_ref, source, flame_ref, image_ref.at[t])

            @pl.when((source >= half) & (source < ready))
            def _(t=t, j=j, source=source):
                add_terms(coefs_of(coef_ref, j), cross_ref, source - half, flame_ref, image_ref.at[t])


def late_kernel(half, rows, slabs, count_offs, ready, offsets_ref, coef_ref, turn_ref, *refs):
    count = 2 * half - ready
    pieces = pair_up(refs[:count], 0)
    sound_ref, high_ref, low_ref, flame_ref, image_in_ref, sums_in_ref = refs[count : count + 6]
    adjoint_refs = refs[count + 6 : count + 6 + half]
    image_refs = refs[count + 6 + half : count + 6 + 2 * half]
    out_ref, site_ref, flat_ref, sums_ref = refs[count + 6 + 2 * half :]
    here = lax.axis_index("order") % half
    places = [half + t for t in cross_order(half)[-count:]]
    operate(pieces, rows, places, turn_ref, sound_ref, high_ref, low_ref, flat_ref, site_ref)
    sums_ref[...] = sums_in_ref[...]
    for t in range(half):
        image_refs[t][...] = image_in_ref[t]
        for j in range(count_offs):
            source = source_of(half, offsets_ref, t, j)

            @pl.when(source >= ready)
            def _(t=t, j=j, source=source):
                coefs = coefs_of(coef_ref, j)
                add_terms(coefs, site_ref, source - ready, flame_ref, image_refs[t])
                inner_products(
                    rows, coefs, site_ref, source - ready, adjoint_refs[t], flame_ref, sums_ref,
                    t * 2 * count_offs + j, t * 2 * count_offs + count_offs + j,
                )

    for t in range(half):
        totals = [
            jnp.sum(sums_ref[t * 2 * count_offs + i], axis=0, keepdims=True)
            for i in range(2 * count_offs)
        ]
        totals = jnp.concatenate(totals, axis=0)
        for slab in range(slabs):
            place = pl.multiple_of(((here ^ t) * slabs + slab) * 8, 8)
            out_ref[pl.ds(place, 8), :] = totals


def couple_kernel(half, rows, count_offs, ready, partners, offsets_ref, coef_ref, own_ref, cross_ref, *refs):
    adjoint_refs = refs[: len(partners)]
    flame_ref, *before_refs, sums_ref = refs[len(partners) :]
    for before_ref in before_refs:
        sums_ref[...] = before_ref[...]
    for adjoint_ref, t in zip(adjoint_refs, partners):
        for j in range(count_offs):
            source = source_of(half, offsets_ref, t, j)

            def product(source_ref, place, adjoint_ref=adjoint_ref, t=t, j=j):
                inner_products(
                    rows, coefs_of(coef_ref, j), source_ref, place, adjoint_ref, flame_ref, sums_ref,
                    t * 2 * count_offs + j, t * 2 * count_offs + count_offs + j,
                )

            @pl.when(source < half)
            def _(product=product, source=source):
                product(own_ref, source)

            @pl.when((source >= half) & (source < ready))
            def _(product=product, source=source):
                product(cross_ref, source - half)


def place_kernel(half, rows, count_offs, scale, *refs):
    piece_refs, parts_ref = refs[:half], refs[half]
    image_ref, out_ref, coupling_ref, sems = refs[half + 1 :]
    here = lax.axis_index("order") % half
    copies = []
    for t in range(half):
        start = pl.multiple_of((here ^ t) * rows, rows)
        copies.append(pltpu.make_async_copy(piece_refs[t], image_ref.at[:, pl.ds(start, rows), :], sems.at[t]))
        copies[-1].start()
    total = jnp.sum(jnp.sum(parts_ref[...], axis=0), axis=1, keepdims=True) * scale
    total = jnp.broadcast_to(total, (8, count_offs))
    row = lax.broadcasted_iota(jnp.int32, (8, count_offs), 0)
    col = lax.broadcasted_iota(jnp.int32, (8, count_offs), 1)
    for part in range(2):
        picked = jnp.where(row == part * count_offs + col, total, 0.0)
        coupling_ref[0, part : part + 1, :] = jnp.sum(picked, axis=0, keepdims=True)
    copies.append(pltpu.make_async_copy(coupling_ref, out_ref, sems.at[half]))
    copies[-1].start()
    for copy in copies:
        copy.wait()


VMEM_SPEC = pl.BlockSpec(memory_space=VMEM)


def call(kernel, ins, spaces, outs, scratch=(), out_specs=None, limit=LIMIT):
    return pl.pallas_call(
        kernel,
        out_shape=outs,
        in_specs=[pl.BlockSpec(memory_space=s) for s in spaces],
        out_specs=jax.tree.map(lambda _: VMEM_SPEC, outs) if out_specs is None else out_specs,
        scratch_shapes=list(scratch),
        compiler_params=pltpu.CompilerParams(vmem_limit_bytes=limit),
    )(*ins)


def local(
    direct, adjoint, sound, transverse, burner_temp, burner_gain, flame_cells, flame_weight, offsets
):
    f32 = jnp.float32
    orders = lax.axis_size("order")
    slabs = lax.axis_size("slab")
    order_now = lax.axis_index("order")
    half = orders // 2
    layers, width = direct.shape[2:]
    mid = width // 2
    rows = layers // half
    count_offs = offsets.shape[0]
    here = order_now % half
    block_rows = 2 * (rows // 8) * 2 * 8 + 8
    ready = orders - LATE

    def of(*shape, dtype=f32):
        return jax.ShapeDtypeStruct(shape, dtype)

    def swap(value, t):
        return lax.ppermute(value, "order", [(i, i ^ t) for i in range(orders)])

    field = direct[0]
    arrivals = cross_order(half)
    bare = arrivals[:BARE]
    *bodies, top, bottom = call(
        functools.partial(first_kernel, half, rows, bare),
        (field, sound),
        (pltpu.HBM, pltpu.HBM),
        [of(2, rows, width)] * BARE + [of(8, mid), of(8, mid)],
        [pltpu.VMEM((2, 8, width), f32), pltpu.VMEM((8, width), f32)] * 2
        + [pltpu.SemaphoreType.DMA((4 + BARE,))],
        limit=None,
    )
    if slabs == 2:
        above = below = lax.ppermute(top, "slab", [(0, 1), (1, 0)])
    else:
        above = lax.ppermute(bottom, "slab", [(i, i + 1) for i in range(slabs - 1)])
        below = lax.ppermute(top, "slab", [(i + 1, i) for i in range(slabs - 1)])

    sent = call(
        functools.partial(pack_kernel, half, rows, bare),
        (field, sound, above, below),
        (VMEM,) * 4,
        [of(block_rows, mid)] * half + [of(8, mid)] * BARE + [of(rows + 8, width)],
    )
    halos, sound_site = sent[half : half + BARE], sent[half + BARE]
    own = [sent[0]] + [swap(sent[t], t) for t in range(1, half)]
    pieces = []
    for t, body, halo in zip(bare, bodies, halos):
        pieces += [swap(body, half ^ t), swap(halo, half ^ t)]
    cross = [swap(sent[t], half ^ t) for t in arrivals[BARE:]]
    pieces += cross[: half - BARE - LATE]

    adjoint_cut = adjoint[0].reshape(2, half, rows, width)
    adj_sent = [lax.dynamic_index_in_dim(adjoint_cut, here ^ t, 1, keepdims=False) for t in range(half)]
    adj = [adj_sent[0]] + [swap(adj_sent[t], t) for t in range(1, half)]

    high, low = call(split_kernel, (transverse,), (VMEM,), [of(*transverse.shape, dtype=jnp.bfloat16)] * 2)
    turn, coef = call(
        functools.partial(table_kernel, orders),
        (offsets, burner_temp.reshape(1, -1), burner_gain.reshape(1, -1)),
        (SMEM, VMEM, VMEM),
        [of(2 * orders, LANES), of(32, LANES)],
    )
    flame = call(
        functools.partial(flame_kernel, half, rows, 4),
        (flame_cells.reshape(-1, LANES), flame_weight.reshape(-1, LANES)),
        (VMEM, VMEM),
        of(rows, width),
    )

    def base(pieces, places, split):
        return call(
            functools.partial(base_kernel, len(places), rows, places, split),
            (turn, *pieces, sound_site, high, low),
            (VMEM,) * (len(pieces) + 4),
            of(len(places), 4, rows, width),
            [pltpu.VMEM((len(places) * 2 * rows, width), f32)],
        )

    site_own = base(own, list(range(half)), 0)
    site_cross = base(pieces, [half + t for t in arrivals[:-LATE]], BARE)
    image_early = call(
        functools.partial(early_kernel, half, count_offs, ready),
        (offsets, coef, site_own, site_cross, flame),
        (SMEM,) + (VMEM,) * 4,
        of(half, 2, rows, width),
    )
    sums_shape = (half * 2 * count_offs, 8, LANES)
    sums_early = ()
    partners = [0] + far_first(half)
    for some in (partners[:-LAST], partners[-LAST:]):
        sums_early = call(
            functools.partial(couple_kernel, half, rows, count_offs, ready, some),
            (offsets, coef, site_own, site_cross, *(adj[t] for t in some), flame, *sums_early),
            (SMEM,) + (VMEM,) * (len(some) + 4 + len(sums_early)),
            [of(*sums_shape)],
        )
    *images, sums = call(
        functools.partial(late_kernel, half, rows, slabs, count_offs, ready),
        (offsets, coef, turn, *cross[half - BARE - LATE :], sound_site, high, low, flame, image_early, *sums_early, *adj),
        (SMEM,) + (VMEM,) * (LATE + half + 8),
        [of(2, rows, width)] * half + [of(half * slabs * 8, LANES)],
        [
            pltpu.VMEM((LATE, 4, rows, width), f32),
            pltpu.VMEM((LATE * 2 * rows, width), f32),
            pltpu.VMEM(sums_shape, f32),
        ],
    )

    back = [images[0]] + [swap(images[t], t) for t in range(1, half)]
    groups = [list(range(half * slabs)), list(range(half * slabs, orders * slabs))]
    parts = lax.all_to_all(
        sums.reshape(half * slabs, 8, LANES), ("order", "slab"), 0, 0, axis_index_groups=groups, tiled=True
    )
    scale = 1.0 / math.sqrt(layers * slabs * width)
    image, coupling = call(
        functools.partial(place_kernel, half, rows, count_offs, scale),
        (*back, parts),
        (VMEM,) * (half + 1),
        [of(2, layers, width), of(1, 2, count_offs)],
        [pltpu.VMEM((1, 2, count_offs), f32), pltpu.SemaphoreType.DMA((half + 1,))],
        [pl.BlockSpec(memory_space=pltpu.HBM)] * 2,
    )
    return (image[None], coupling)


def far_first(half):
    return sorted(range(1, half), key=lambda t: (-bin(t >> 1).count("1"), t & 1 if t > 1 else 2, -t))


def solution(mesh):
    in_specs = (
        P("order", None, "slab", None),
        P("order", None, "slab", None),
        P("slab", None),
        P(),
        P(),
        P(),
        P(),
        P(),
        P(),
    )
    out_specs = (P("order", None, "slab", None), P("order", None, None))

    return jax.shard_map(local, mesh=mesh, in_specs=in_specs, out_specs=out_specs, check_vma=False)
```

```python
import functools
import math

import jax
import jax.numpy as jnp
from jax import lax
from jax.experimental import pallas as pl
from jax.experimental.pallas import tpu as pltpu
from jax.sharding import PartitionSpec as P


VMEM = pltpu.VMEM
SMEM = pltpu.SMEM
LANES = 128
LATE = 2
BARE = 2
LAST = 2
LIMIT = 20 * 1024 * 1024


def first_kernel(half, rows, partners, direct_ref, sound_ref, *refs):
    body_refs = refs[: len(partners)]
    top_ref, bottom_ref, *block_refs, sems = refs[len(partners) :]
    layers, width = sound_ref.shape
    mid = width // 2
    here = lax.axis_index("order") % half
    copies = []

    def begin(source, target):
        copies.append(pltpu.make_async_copy(source, target, sems.at[len(copies)]))
        copies[-1].start()

    for i, low in enumerate((0, layers - 8)):
        begin(direct_ref.at[:, pl.ds(low, 8), :], block_refs[2 * i])
        begin(sound_ref.at[pl.ds(low, 8), :], block_refs[2 * i + 1])
    for t, body_ref in zip(partners, body_refs):
        start = pl.multiple_of((here ^ t) * rows, rows)
        begin(direct_ref.at[:, pl.ds(start, rows), :], body_ref)
    for copy in copies[:4]:
        copy.wait()
    for i, (out_ref, row) in enumerate(((top_ref, 0), (bottom_ref, 7))):
        for part in range(2):
            for side in range(2):
                out_ref[2 * part + side, :] = block_refs[2 * i][part, row, side * mid : (side + 1) * mid]
        for side in range(2):
            out_ref[4 + side, :] = block_refs[2 * i + 1][row, side * mid : (side + 1) * mid]
            out_ref[6 + side, :] = jnp.zeros((mid,), jnp.float32)
    if lax.axis_size("slab") == 2:
        top_ref[...] = jnp.where(lax.axis_index("slab") == 0, bottom_ref[...], top_ref[...])
    for copy in copies[4:]:
        copy.wait()


def pack_kernel(half, rows, bare, field_ref, sound_ref, above_ref, below_ref, *out_refs):
    here = lax.axis_index("order") % half
    slab = lax.axis_index("slab")
    has_above, has_below = slab > 0, slab < lax.axis_size("slab") - 1
    width = field_ref.shape[2]
    mid = width // 2
    for t in range(half):
        site = here ^ t
        start = pl.multiple_of(site * rows, rows)
        block = 0
        for part in range(2):
            for low in range(0, rows, 8):
                for side in range(2):
                    out_refs[t][block * 8 : block * 8 + 8, :] = field_ref[
                        part, pl.ds(start + low, 8), side * mid : (side + 1) * mid
                    ]
                    block += 1
        before = jnp.maximum(start - 1, 0)
        after = jnp.minimum(start + rows, half * rows - 1)
        for part in range(2):
            for side in range(2):
                cut = slice(side * mid, (side + 1) * mid)
                from_slab = 2 * part + side
                edge = jnp.where(has_above, above_ref[from_slab : from_slab + 1, :], 0.0)
                up = jnp.where(site == 0, edge, field_ref[part, pl.ds(before, 1), cut])
                edge = jnp.where(has_below, below_ref[from_slab : from_slab + 1, :], 0.0)
                down = jnp.where(site == half - 1, edge, field_ref[part, pl.ds(after, 1), cut])
                for place, value in enumerate((up, down)):
                    at = part * 4 + place * 2 + side
                    out_refs[t][block * 8 + at : block * 8 + at + 1, :] = value
                    if t in bare:
                        out_refs[half + bare.index(t)][at : at + 1, :] = value
    site_ref = out_refs[half + len(bare)]
    start = pl.multiple_of(here * rows, rows)
    site_ref[0:rows, :] = sound_ref[pl.ds(start, rows), :]
    before = jnp.maximum(start - 1, 0)
    after = jnp.minimum(start + rows, half * rows - 1)
    for side in range(2):
        cut = slice(side * mid, (side + 1) * mid)
        edge = jnp.where(has_above, above_ref[4 + side : 5 + side, :], 0.0)
        site_ref[rows : rows + 1, cut] = jnp.where(here == 0, edge, sound_ref[pl.ds(before, 1), cut])
        edge = jnp.where(has_below, below_ref[4 + side : 5 + side, :], 0.0)
        site_ref[rows + 1 : rows + 2, cut] = jnp.where(here == half - 1, edge, sound_ref[pl.ds(after, 1), cut])


def table_kernel(orders, offsets_ref, temp_ref, gain_ref, turn_ref, coef_ref):
    step = 2.0 * math.pi / orders
    own = lax.axis_index("order")
    ids = lax.broadcasted_iota(jnp.int32, (orders, LANES), 0) ^ own
    angles = step * ids.astype(jnp.float32)
    turn_ref[0:orders, :] = jnp.cos(angles)
    turn_ref[orders:, :] = jnp.sin(angles)
    row = lax.broadcasted_iota(jnp.int32, (8, orders), 0)
    offset = jnp.zeros((8, orders), jnp.int32)
    for j in range(offsets_ref.shape[0]):
        offset = jnp.where(row == j, offsets_ref[j], offset)
    turns = (offset * lax.broadcasted_iota(jnp.int32, (8, orders), 1)) & (orders - 1)
    angles = step * turns.astype(jnp.float32)
    cos, sin = jnp.cos(angles), jnp.sin(angles)
    for p, (values_ref, wave, sign) in enumerate(
        ((temp_ref, cos, 1.0), (temp_ref, sin, -1.0), (gain_ref, cos, 1.0), (gain_ref, sin, -1.0))
    ):
        total = sign * jnp.sum(values_ref[...] * wave, axis=1, keepdims=True) / orders
        coef_ref[8 * p : 8 * p + 8, :] = jnp.broadcast_to(total, (8, LANES))


def split_kernel(full_ref, high_ref, low_ref):
    full = full_ref[...]
    high = full.astype(jnp.bfloat16)
    high_ref[...] = high
    low_ref[...] = (full - high.astype(jnp.float32)).astype(jnp.bfloat16)


def flame_kernel(half, rows, step, cells_ref, weight_ref, out_ref):
    width = out_ref.shape[1]
    shift = width.bit_length() - 1
    first = lax.axis_index("slab") * (half * rows) + lax.axis_index("order") % half * rows
    total = jnp.zeros((3 * rows, width), jnp.float32)
    for at in range(0, cells_ref.shape[0], step):
        cells = jnp.concatenate([cells_ref[i : i + 1, :] for i in range(at, at + step)], axis=1)
        weight = jnp.concatenate([weight_ref[i : i + 1, :] for i in range(at, at + step)], axis=1)
        cell_row = (cells >> shift) - first
        cell_col = cells & (width - 1)
        one = weight.astype(jnp.bfloat16).astype(jnp.float32)
        two = (weight - one).astype(jnp.bfloat16).astype(jnp.float32)
        three = weight - one - two
        hit = lax.broadcasted_iota(jnp.int32, (rows, step * LANES), 0) == cell_row
        left = jnp.concatenate([jnp.where(hit, x, 0.0) for x in (one, two, three)], axis=0)
        right = jnp.where(lax.broadcasted_iota(jnp.int32, (width, step * LANES), 0) == cell_col, 1.0, 0.0)
        total += lax.dot_general(
            left.astype(jnp.bfloat16),
            right.astype(jnp.bfloat16),
            (((1,), (1,)), ((), ())),
            preferred_element_type=jnp.float32,
        )
    out_ref[...] = total[:rows] + total[rows : 2 * rows] + total[2 * rows :]


def fill_flat(pieces, rows, flat_ref):
    mid = flat_ref.shape[1] // 2
    for i, (body_ref, _) in enumerate(pieces):
        first = i * 2 * rows
        if len(body_ref.shape) == 3:
            flat_ref[first : first + rows, :] = body_ref[0]
            flat_ref[first + rows : first + 2 * rows, :] = body_ref[1]
            continue
        block = 0
        for low in range(0, 2 * rows, 8):
            for side in range(2):
                flat_ref[first + low : first + low + 8, side * mid : (side + 1) * mid] = body_ref[
                    block * 8 : block * 8 + 8, :
                ]
                block += 1


def operate(pieces, rows, places, turn_ref, sound_ref, high_ref, low_ref, flat_ref, out_ref):
    width = sound_ref.shape[1]
    stacks = 2 * rows
    fill_flat(pieces, rows, flat_ref)
    flat = flat_ref[...]
    high = flat.astype(jnp.bfloat16)
    low_part = (flat - high.astype(jnp.float32)).astype(jnp.bfloat16)

    def dot(a, b):
        return jnp.dot(a, b, preferred_element_type=jnp.float32)

    both = dot(jnp.concatenate([high, low_part], axis=0), high_ref[...])
    across = both[: flat.shape[0]] + (dot(high, low_ref[...]) + both[flat.shape[0] :])
    orders = turn_ref.shape[0] // 2
    middle = sound_ref[0:rows, :]
    sound_up = jnp.concatenate([sound_ref[rows : rows + 1, :], middle[: rows - 1]], axis=0)
    sound_down = jnp.concatenate([middle[1:], sound_ref[rows + 1 : rows + 2, :]], axis=0)
    weight_up = 0.5 * (middle + sound_up)
    weight_down = 0.5 * (middle + sound_down)
    seam = 0.5 * (middle[:, width - 1 : width] + middle[:, 0:1])
    lane = lax.broadcasted_iota(jnp.int32, (rows, width), 1)
    for i, (_, halo_ref) in enumerate(pieces):
        at = places[i]
        cos_turn = turn_ref[at : at + 1, 0:1]
        sin_turn = turn_ref[orders + at : orders + at + 1, 0:1]
        fields = []
        for part in range(2):
            fields.append(flat[i * stacks + part * rows : i * stacks + (part + 1) * rows])
        firsts = [f[:, 0:1] for f in fields]
        lasts = [f[:, width - 1 : width] for f in fields]
        ahead = (
            cos_turn * firsts[0] - sin_turn * firsts[1],
            sin_turn * firsts[0] + cos_turn * firsts[1],
        )
        behind = (
            cos_turn * lasts[0] + sin_turn * lasts[1],
            cos_turn * lasts[1] - sin_turn * lasts[0],
        )
        halo_rows = halo_ref[halo_ref.shape[0] - 8 :, :]
        for part in range(2):
            field = fields[part]
            halo = halo_rows[part * 4 : part * 4 + 4]
            up = jnp.concatenate([halo[0:1], halo[1:2]], axis=1)
            down = jnp.concatenate([halo[2:3], halo[3:4]], axis=1)
            above = jnp.concatenate([up, field[: rows - 1]], axis=0)
            below = jnp.concatenate([field[1:], down], axis=0)
            result = weight_down * (field - below) + weight_up * (field - above)
            result = result + across[i * stacks + part * rows : i * stacks + (part + 1) * rows]
            last_add = seam * (lasts[part] - ahead[part])
            first_add = seam * (firsts[part] - behind[part])
            result = result + jnp.where(lane == width - 1, last_add, 0.0)
            result = result + jnp.where(lane == 0, first_add, 0.0)
            out_ref[i, part] = result
            out_ref[i, 2 + part] = field


def pair_up(refs, split):
    apart = [(refs[2 * i], refs[2 * i + 1]) for i in range(split)]
    return apart + [(r, r) for r in refs[2 * split :]]


def base_kernel(count, rows, places, split, turn_ref, *refs):
    taken = count + split
    pieces = pair_up(refs[:taken], split)
    sound_ref, high_ref, low_ref = refs[taken : taken + 3]
    out_ref, flat_ref = refs[-2:]
    operate(pieces, rows, places, turn_ref, sound_ref, high_ref, low_ref, flat_ref, out_ref)


def add_terms(coefs, source_ref, source, flame_ref, image_ref):
    temp_re, temp_im, gain_re, gain_im = coefs
    for at in range(0, flame_ref.shape[1], LANES):
        cut = slice(at, at + LANES)
        flame = flame_ref[:, cut]
        base_re = source_ref[source, 0, :, cut]
        base_im = source_ref[source, 1, :, cut]
        field_re = source_ref[source, 2, :, cut]
        field_im = source_ref[source, 3, :, cut]
        image_ref[0, :, cut] += (
            temp_re * base_re - temp_im * base_im + flame * (gain_re * field_re - gain_im * field_im)
        )
        image_ref[1, :, cut] += (
            temp_re * base_im + temp_im * base_re + flame * (gain_re * field_im + gain_im * field_re)
        )


def inner_products(rows, coefs, source_ref, source, adjoint_ref, flame_ref, sums_ref, at_re, at_im):
    temp_re, temp_im, gain_re, gain_im = coefs

    def fold(x):
        out = x[0:8]
        for low in range(8, rows, 8):
            out = out + x[low : low + 8]
        return out

    sums = [jnp.zeros((8, LANES), jnp.float32)] * 4
    for at in range(0, flame_ref.shape[1], LANES):
        cut = slice(at, at + LANES)
        flame = flame_ref[:, cut]
        adj_re = adjoint_ref[0, :, cut]
        adj_im = adjoint_ref[1, :, cut]
        base_re = source_ref[source, 0, :, cut]
        base_im = source_ref[source, 1, :, cut]
        field_re = flame * source_ref[source, 2, :, cut]
        field_im = flame * source_ref[source, 3, :, cut]
        sums[0] = sums[0] + fold(adj_re * base_re + adj_im * base_im)
        sums[1] = sums[1] + fold(adj_re * base_im - adj_im * base_re)
        sums[2] = sums[2] + fold(adj_re * field_re + adj_im * field_im)
        sums[3] = sums[3] + fold(adj_re * field_im - adj_im * field_re)
    sums_ref[at_re] = temp_re * sums[0] - temp_im * sums[1] + gain_re * sums[2] - gain_im * sums[3]
    sums_ref[at_im] = temp_re * sums[1] + temp_im * sums[0] + gain_re * sums[3] + gain_im * sums[2]


def coefs_of(coef_ref, j):
    return tuple(coef_ref[8 * p + j : 8 * p + j + 1, :] for p in range(4))


def source_of(half, offsets_ref, t, j):
    own = lax.axis_index("order")
    orders = 2 * half
    place = (((own ^ t) - offsets_ref[j] + orders) & (orders - 1)) ^ own
    quarter = half // 2
    later = half + (place & (quarter - 1)) * 2 + ((place & quarter) // quarter)
    return jnp.where(place < half, place, later)


def cross_order(half):
    return [t + far for t in range(half // 2) for far in (0, half // 2)]


def early_kernel(half, count_offs, ready, offsets_ref, coef_ref, own_ref, cross_ref, flame_ref, image_ref):
    for t in range(half):
        image_ref[t, 0] = own_ref[t, 0]
        image_ref[t, 1] = own_ref[t, 1]
        for j in range(count_offs):
            source = source_of(half, offsets_ref, t, j)

            @pl.when(source < half)
            def _(t=t, j=j, source=source):
                add_terms(coefs_of(coef_ref, j), own_ref, source, flame_ref, image_ref.at[t])

            @pl.when((source >= half) & (source < ready))
            def _(t=t, j=j, source=source):
                add_terms(coefs_of(coef_ref, j), cross_ref, source - half, flame_ref, image_ref.at[t])


def late_kernel(half, rows, slabs, count_offs, ready, offsets_ref, coef_ref, turn_ref, *refs):
    count = 2 * half - ready
    pieces = pair_up(refs[:count], 0)
    sound_ref, high_ref, low_ref, flame_ref, image_in_ref, sums_in_ref = refs[count : count + 6]
    adjoint_refs = refs[count + 6 : count + 6 + half]
    image_refs = refs[count + 6 + half : count + 6 + 2 * half]
    out_ref, site_ref, flat_ref, sums_ref = refs[count + 6 + 2 * half :]
    here = lax.axis_index("order") % half
    places = [half + t for t in cross_order(half)[-count:]]
    operate(pieces, rows, places, turn_ref, sound_ref, high_ref, low_ref, flat_ref, site_ref)
    sums_ref[...] = sums_in_ref[...]
    for t in range(half):
        image_refs[t][...] = image_in_ref[t]
        for j in range(count_offs):
            source = source_of(half, offsets_ref, t, j)

            @pl.when(source >= ready)
            def _(t=t, j=j, source=source):
                coefs = coefs_of(coef_ref, j)
                add_terms(coefs, site_ref, source - ready, flame_ref, image_refs[t])
                inner_products(
                    rows, coefs, site_ref, source - ready, adjoint_refs[t], flame_ref, sums_ref,
                    t * 2 * count_offs + j, t * 2 * count_offs + count_offs + j,
                )

    for t in range(half):
        totals = [
            jnp.sum(sums_ref[t * 2 * count_offs + i], axis=0, keepdims=True)
            for i in range(2 * count_offs)
        ]
        totals = jnp.concatenate(totals, axis=0)
        for slab in range(slabs):
            place = pl.multiple_of(((here ^ t) * slabs + slab) * 8, 8)
            out_ref[pl.ds(place, 8), :] = totals


def couple_kernel(half, rows, count_offs, ready, partners, offsets_ref, coef_ref, own_ref, cross_ref, *refs):
    adjoint_refs = refs[: len(partners)]
    flame_ref, *before_refs, sums_ref = refs[len(partners) :]
    for before_ref in before_refs:
        sums_ref[...] = before_ref[...]
    for adjoint_ref, t in zip(adjoint_refs, partners):
        for j in range(count_offs):
            source = source_of(half, offsets_ref, t, j)

            def product(source_ref, place, adjoint_ref=adjoint_ref, t=t, j=j):
                inner_products(
                    rows, coefs_of(coef_ref, j), source_ref, place, adjoint_ref, flame_ref, sums_ref,
                    t * 2 * count_offs + j, t * 2 * count_offs + count_offs + j,
                )

            @pl.when(source < half)
            def _(product=product, source=source):
                product(own_ref, source)

            @pl.when((source >= half) & (source < ready))
            def _(product=product, source=source):
                product(cross_ref, source - half)


def place_kernel(half, rows, count_offs, scale, *refs):
    piece_refs, parts_ref = refs[:half], refs[half]
    image_ref, out_ref, coupling_ref, sems = refs[half + 1 :]
    here = lax.axis_index("order") % half
    copies = []
    for t in range(half):
        start = pl.multiple_of((here ^ t) * rows, rows)
        copies.append(pltpu.make_async_copy(piece_refs[t], image_ref.at[:, pl.ds(start, rows), :], sems.at[t]))
        copies[-1].start()
    total = jnp.sum(jnp.sum(parts_ref[...], axis=0), axis=1, keepdims=True) * scale
    total = jnp.broadcast_to(total, (8, count_offs))
    row = lax.broadcasted_iota(jnp.int32, (8, count_offs), 0)
    col = lax.broadcasted_iota(jnp.int32, (8, count_offs), 1)
    for part in range(2):
        picked = jnp.where(row == part * count_offs + col, total, 0.0)
        coupling_ref[0, part : part + 1, :] = jnp.sum(picked, axis=0, keepdims=True)
    copies.append(pltpu.make_async_copy(coupling_ref, out_ref, sems.at[half]))
    copies[-1].start()
    for copy in copies:
        copy.wait()


VMEM_SPEC = pl.BlockSpec(memory_space=VMEM)


def call(kernel, ins, spaces, outs, scratch=(), out_specs=None, limit=LIMIT):
    return pl.pallas_call(
        kernel,
        out_shape=outs,
        in_specs=[pl.BlockSpec(memory_space=s) for s in spaces],
        out_specs=jax.tree.map(lambda _: VMEM_SPEC, outs) if out_specs is None else out_specs,
        scratch_shapes=list(scratch),
        compiler_params=pltpu.CompilerParams(vmem_limit_bytes=limit),
    )(*ins)


def local(
    direct, adjoint, sound, transverse, burner_temp, burner_gain, flame_cells, flame_weight, offsets
):
    f32 = jnp.float32
    orders = lax.axis_size("order")
    slabs = lax.axis_size("slab")
    order_now = lax.axis_index("order")
    half = orders // 2
    layers, width = direct.shape[2:]
    mid = width // 2
    rows = layers // half
    count_offs = offsets.shape[0]
    here = order_now % half
    block_rows = 2 * (rows // 8) * 2 * 8 + 8
    ready = orders - LATE

    def of(*shape, dtype=f32):
        return jax.ShapeDtypeStruct(shape, dtype)

    def swap(value, t):
        return lax.ppermute(value, "order", [(i, i ^ t) for i in range(orders)])

    field = direct[0]
    arrivals = cross_order(half)
    bare = arrivals[:BARE]
    *bodies, top, bottom = call(
        functools.partial(first_kernel, half, rows, bare),
        (field, sound),
        (pltpu.HBM, pltpu.HBM),
        [of(2, rows, width)] * BARE + [of(8, mid), of(8, mid)],
        [pltpu.VMEM((2, 8, width), f32), pltpu.VMEM((8, width), f32)] * 2
        + [pltpu.SemaphoreType.DMA((4 + BARE,))],
        limit=None,
    )
    if slabs == 2:
        above = below = lax.ppermute(top, "slab", [(0, 1), (1, 0)])
    else:
        above = lax.ppermute(bottom, "slab", [(i, i + 1) for i in range(slabs - 1)])
        below = lax.ppermute(top, "slab", [(i + 1, i) for i in range(slabs - 1)])

    sent = call(
        functools.partial(pack_kernel, half, rows, bare),
        (field, sound, above, below),
        (VMEM,) * 4,
        [of(block_rows, mid)] * half + [of(8, mid)] * BARE + [of(rows + 8, width)],
    )
    halos, sound_site = sent[half : half + BARE], sent[half + BARE]
    own = [sent[0]] + [swap(sent[t], t) for t in range(1, half)]
    pieces = []
    for t, body, halo in zip(bare, bodies, halos):
        pieces += [swap(body, half ^ t), swap(halo, half ^ t)]
    cross = [swap(sent[t], half ^ t) for t in arrivals[BARE:]]
    pieces += cross[: half - BARE - LATE]

    adjoint_cut = adjoint[0].reshape(2, half, rows, width)
    adj_sent = [lax.dynamic_index_in_dim(adjoint_cut, here ^ t, 1, keepdims=False) for t in range(half)]
    adj = [adj_sent[0]] + [swap(adj_sent[t], t) for t in range(1, half)]

    high, low = call(split_kernel, (transverse,), (VMEM,), [of(*transverse.shape, dtype=jnp.bfloat16)] * 2)
    turn, coef = call(
        functools.partial(table_kernel, orders),
        (offsets, burner_temp.reshape(1, -1), burner_gain.reshape(1, -1)),
        (SMEM, VMEM, VMEM),
        [of(2 * orders, LANES), of(32, LANES)],
    )
    flame = call(
        functools.partial(flame_kernel, half, rows, 4),
        (flame_cells.reshape(-1, LANES), flame_weight.reshape(-1, LANES)),
        (VMEM, VMEM),
        of(rows, width),
    )

    def base(pieces, places, split):
        return call(
            functools.partial(base_kernel, len(places), rows, places, split),
            (turn, *pieces, sound_site, high, low),
            (VMEM,) * (len(pieces) + 4),
            of(len(places), 4, rows, width),
            [pltpu.VMEM((len(places) * 2 * rows, width), f32)],
        )

    site_own = base(own, list(range(half)), 0)
    site_cross = base(pieces, [half + t for t in arrivals[:-LATE]], BARE)
    image_early = call(
        functools.partial(early_kernel, half, count_offs, ready),
        (offsets, coef, site_own, site_cross, flame),
        (SMEM,) + (VMEM,) * 4,
        of(half, 2, rows, width),
    )
    sums_shape = (half * 2 * count_offs, 8, LANES)
    sums_early = ()
    partners = [0] + sorted(even_first(half), key=lambda t: t & 1 and t >= half // 2)
    for some in (partners[:-LAST], partners[-LAST:]):
        sums_early = call(
            functools.partial(couple_kernel, half, rows, count_offs, ready, some),
            (offsets, coef, site_own, site_cross, *(adj[t] for t in some), flame, *sums_early),
            (SMEM,) + (VMEM,) * (len(some) + 4 + len(sums_early)),
            [of(*sums_shape)],
        )
    *images, sums = call(
        functools.partial(late_kernel, half, rows, slabs, count_offs, ready),
        (offsets, coef, turn, *cross[half - BARE - LATE :], sound_site, high, low, flame, image_early, *sums_early, *adj),
        (SMEM,) + (VMEM,) * (LATE + half + 8),
        [of(2, rows, width)] * half + [of(half * slabs * 8, LANES)],
        [
            pltpu.VMEM((LATE, 4, rows, width), f32),
            pltpu.VMEM((LATE * 2 * rows, width), f32),
            pltpu.VMEM(sums_shape, f32),
        ],
    )

    back = [images[0]] + [swap(images[t], t) for t in range(1, half)]
    groups = [list(range(half * slabs)), list(range(half * slabs, orders * slabs))]
    parts = lax.all_to_all(
        sums.reshape(half * slabs, 8, LANES), ("order", "slab"), 0, 0, axis_index_groups=groups, tiled=True
    )
    scale = 1.0 / math.sqrt(layers * slabs * width)
    image, coupling = call(
        functools.partial(place_kernel, half, rows, count_offs, scale),
        (*back, parts),
        (VMEM,) * (half + 1),
        [of(2, layers, width), of(1, 2, count_offs)],
        [pltpu.VMEM((1, 2, count_offs), f32), pltpu.SemaphoreType.DMA((half + 1,))],
        [pl.BlockSpec(memory_space=pltpu.HBM)] * 2,
    )
    return (image[None], coupling)


def even_first(half):
    return sorted(range(1, half), key=lambda t: (t & 1, -t))


def solution(mesh):
    in_specs = (
        P("order", None, "slab", None),
        P("order", None, "slab", None),
        P("slab", None),
        P(),
        P(),
        P(),
        P(),
        P(),
        P(),
    )
    out_specs = (P("order", None, "slab", None), P("order", None, None))

    return jax.shard_map(local, mesh=mesh, in_specs=in_specs, out_specs=out_specs, check_vma=False)
```

```python
import functools
import math

import jax
import jax.numpy as jnp
from jax import lax
from jax.experimental import pallas as pl
from jax.experimental.pallas import tpu as pltpu
from jax.sharding import PartitionSpec as P


VMEM = pltpu.VMEM
SMEM = pltpu.SMEM
LANES = 128
LATE = 2
BARE = 1
LAST = 2
LIMIT = 20 * 1024 * 1024


def first_kernel(half, rows, partners, direct_ref, sound_ref, *refs):
    body_refs = refs[: len(partners)]
    top_ref, bottom_ref, *block_refs, sems = refs[len(partners) :]
    layers, width = sound_ref.shape
    mid = width // 2
    here = lax.axis_index("order") % half
    copies = []

    def begin(source, target):
        copies.append(pltpu.make_async_copy(source, target, sems.at[len(copies)]))
        copies[-1].start()

    for i, low in enumerate((0, layers - 8)):
        begin(direct_ref.at[:, pl.ds(low, 8), :], block_refs[2 * i])
        begin(sound_ref.at[pl.ds(low, 8), :], block_refs[2 * i + 1])
    for t, body_ref in zip(partners, body_refs):
        start = pl.multiple_of((here ^ t) * rows, rows)
        begin(direct_ref.at[:, pl.ds(start, rows), :], body_ref)
    for copy in copies[:4]:
        copy.wait()
    for i, (out_ref, row) in enumerate(((top_ref, 0), (bottom_ref, 7))):
        for part in range(2):
            for side in range(2):
                out_ref[2 * part + side, :] = block_refs[2 * i][part, row, side * mid : (side + 1) * mid]
        for side in range(2):
            out_ref[4 + side, :] = block_refs[2 * i + 1][row, side * mid : (side + 1) * mid]
            out_ref[6 + side, :] = jnp.zeros((mid,), jnp.float32)
    if lax.axis_size("slab") == 2:
        top_ref[...] = jnp.where(lax.axis_index("slab") == 0, bottom_ref[...], top_ref[...])
    for copy in copies[4:]:
        copy.wait()


def pack_kernel(half, rows, bare, field_ref, above_ref, below_ref, *out_refs):
    here = lax.axis_index("order") % half
    slab = lax.axis_index("slab")
    has_above, has_below = slab > 0, slab < lax.axis_size("slab") - 1
    width = field_ref.shape[2]
    mid = width // 2
    for t in range(half):
        site = here ^ t
        start = pl.multiple_of(site * rows, rows)
        block = 0
        for part in range(2):
            for low in range(0, rows, 8):
                for side in range(2):
                    out_refs[t][block * 8 : block * 8 + 8, :] = field_ref[
                        part, pl.ds(start + low, 8), side * mid : (side + 1) * mid
                    ]
                    block += 1
        before = jnp.maximum(start - 1, 0)
        after = jnp.minimum(start + rows, half * rows - 1)
        for part in range(2):
            for side in range(2):
                cut = slice(side * mid, (side + 1) * mid)
                from_slab = 2 * part + side
                edge = jnp.where(has_above, above_ref[from_slab : from_slab + 1, :], 0.0)
                up = jnp.where(site == 0, edge, field_ref[part, pl.ds(before, 1), cut])
                edge = jnp.where(has_below, below_ref[from_slab : from_slab + 1, :], 0.0)
                down = jnp.where(site == half - 1, edge, field_ref[part, pl.ds(after, 1), cut])
                for place, value in enumerate((up, down)):
                    at = part * 4 + place * 2 + side
                    out_refs[t][block * 8 + at : block * 8 + at + 1, :] = value
                    if t in bare:
                        out_refs[half + bare.index(t)][at : at + 1, :] = value


def sound_kernel(half, rows, sound_ref, above_ref, below_ref, site_ref):
    here = lax.axis_index("order") % half
    slab = lax.axis_index("slab")
    has_above, has_below = slab > 0, slab < lax.axis_size("slab") - 1
    mid = sound_ref.shape[1] // 2
    start = pl.multiple_of(here * rows, rows)
    site_ref[0:rows, :] = sound_ref[pl.ds(start, rows), :]
    before = jnp.maximum(start - 1, 0)
    after = jnp.minimum(start + rows, half * rows - 1)
    for side in range(2):
        cut = slice(side * mid, (side + 1) * mid)
        edge = jnp.where(has_above, above_ref[4 + side : 5 + side, :], 0.0)
        site_ref[rows : rows + 1, cut] = jnp.where(here == 0, edge, sound_ref[pl.ds(before, 1), cut])
        edge = jnp.where(has_below, below_ref[4 + side : 5 + side, :], 0.0)
        site_ref[rows + 1 : rows + 2, cut] = jnp.where(here == half - 1, edge, sound_ref[pl.ds(after, 1), cut])


def table_kernel(orders, offsets_ref, temp_ref, gain_ref, turn_ref, coef_ref):
    step = 2.0 * math.pi / orders
    own = lax.axis_index("order")
    ids = lax.broadcasted_iota(jnp.int32, (orders, LANES), 0) ^ own
    angles = step * ids.astype(jnp.float32)
    turn_ref[0:orders, :] = jnp.cos(angles)
    turn_ref[orders:, :] = jnp.sin(angles)
    row = lax.broadcasted_iota(jnp.int32, (8, orders), 0)
    offset = jnp.zeros((8, orders), jnp.int32)
    for j in range(offsets_ref.shape[0]):
        offset = jnp.where(row == j, offsets_ref[j], offset)
    turns = (offset * lax.broadcasted_iota(jnp.int32, (8, orders), 1)) & (orders - 1)
    angles = step * turns.astype(jnp.float32)
    cos, sin = jnp.cos(angles), jnp.sin(angles)
    for p, (values_ref, wave, sign) in enumerate(
        ((temp_ref, cos, 1.0), (temp_ref, sin, -1.0), (gain_ref, cos, 1.0), (gain_ref, sin, -1.0))
    ):
        total = sign * jnp.sum(values_ref[...] * wave, axis=1, keepdims=True) / orders
        coef_ref[8 * p : 8 * p + 8, :] = jnp.broadcast_to(total, (8, LANES))


def split_kernel(full_ref, high_ref, low_ref):
    full = full_ref[...]
    high = full.astype(jnp.bfloat16)
    high_ref[...] = high
    low_ref[...] = (full - high.astype(jnp.float32)).astype(jnp.bfloat16)


def flame_kernel(half, rows, step, cells_ref, weight_ref, out_ref):
    width = out_ref.shape[1]
    shift = width.bit_length() - 1
    first = lax.axis_index("slab") * (half * rows) + lax.axis_index("order") % half * rows
    total = jnp.zeros((3 * rows, width), jnp.float32)
    for at in range(0, cells_ref.shape[0], step):
        cells = jnp.concatenate([cells_ref[i : i + 1, :] for i in range(at, at + step)], axis=1)
        weight = jnp.concatenate([weight_ref[i : i + 1, :] for i in range(at, at + step)], axis=1)
        cell_row = (cells >> shift) - first
        cell_col = cells & (width - 1)
        one = weight.astype(jnp.bfloat16).astype(jnp.float32)
        two = (weight - one).astype(jnp.bfloat16).astype(jnp.float32)
        three = weight - one - two
        hit = lax.broadcasted_iota(jnp.int32, (rows, step * LANES), 0) == cell_row
        left = jnp.concatenate([jnp.where(hit, x, 0.0) for x in (one, two, three)], axis=0)
        right = jnp.where(lax.broadcasted_iota(jnp.int32, (width, step * LANES), 0) == cell_col, 1.0, 0.0)
        total += lax.dot_general(
            left.astype(jnp.bfloat16),
            right.astype(jnp.bfloat16),
            (((1,), (1,)), ((), ())),
            preferred_element_type=jnp.float32,
        )
    out_ref[...] = total[:rows] + total[rows : 2 * rows] + total[2 * rows :]


def fill_flat(pieces, rows, flat_ref):
    mid = flat_ref.shape[1] // 2
    for i, (body_ref, _) in enumerate(pieces):
        first = i * 2 * rows
        if len(body_ref.shape) == 3:
            flat_ref[first : first + rows, :] = body_ref[0]
            flat_ref[first + rows : first + 2 * rows, :] = body_ref[1]
            continue
        block = 0
        for low in range(0, 2 * rows, 8):
            for side in range(2):
                flat_ref[first + low : first + low + 8, side * mid : (side + 1) * mid] = body_ref[
                    block * 8 : block * 8 + 8, :
                ]
                block += 1


def operate(pieces, rows, places, turn_ref, sound_ref, high_ref, low_ref, flat_ref, out_ref):
    width = sound_ref.shape[1]
    stacks = 2 * rows
    fill_flat(pieces, rows, flat_ref)
    flat = flat_ref[...]
    high = flat.astype(jnp.bfloat16)
    low_part = (flat - high.astype(jnp.float32)).astype(jnp.bfloat16)

    def dot(a, b):
        return jnp.dot(a, b, preferred_element_type=jnp.float32)

    both = dot(jnp.concatenate([high, low_part], axis=0), high_ref[...])
    across = both[: flat.shape[0]] + (dot(high, low_ref[...]) + both[flat.shape[0] :])
    orders = turn_ref.shape[0] // 2
    middle = sound_ref[0:rows, :]
    sound_up = jnp.concatenate([sound_ref[rows : rows + 1, :], middle[: rows - 1]], axis=0)
    sound_down = jnp.concatenate([middle[1:], sound_ref[rows + 1 : rows + 2, :]], axis=0)
    weight_up = 0.5 * (middle + sound_up)
    weight_down = 0.5 * (middle + sound_down)
    seam = 0.5 * (middle[:, width - 1 : width] + middle[:, 0:1])
    lane = lax.broadcasted_iota(jnp.int32, (rows, width), 1)
    for i, (_, halo_ref) in enumerate(pieces):
        at = places[i]
        cos_turn = turn_ref[at : at + 1, 0:1]
        sin_turn = turn_ref[orders + at : orders + at + 1, 0:1]
        fields = []
        for part in range(2):
            fields.append(flat[i * stacks + part * rows : i * stacks + (part + 1) * rows])
        firsts = [f[:, 0:1] for f in fields]
        lasts = [f[:, width - 1 : width] for f in fields]
        ahead = (
            cos_turn * firsts[0] - sin_turn * firsts[1],
            sin_turn * firsts[0] + cos_turn * firsts[1],
        )
        behind = (
            cos_turn * lasts[0] + sin_turn * lasts[1],
            cos_turn * lasts[1] - sin_turn * lasts[0],
        )
        halo_rows = halo_ref[halo_ref.shape[0] - 8 :, :]
        for part in range(2):
            field = fields[part]
            halo = halo_rows[part * 4 : part * 4 + 4]
            up = jnp.concatenate([halo[0:1], halo[1:2]], axis=1)
            down = jnp.concatenate([halo[2:3], halo[3:4]], axis=1)
            above = jnp.concatenate([up, field[: rows - 1]], axis=0)
            below = jnp.concatenate([field[1:], down], axis=0)
            result = weight_down * (field - below) + weight_up * (field - above)
            result = result + across[i * stacks + part * rows : i * stacks + (part + 1) * rows]
            last_add = seam * (lasts[part] - ahead[part])
            first_add = seam * (firsts[part] - behind[part])
            result = result + jnp.where(lane == width - 1, last_add, 0.0)
            result = result + jnp.where(lane == 0, first_add, 0.0)
            out_ref[i, part] = result
            out_ref[i, 2 + part] = field


def pair_up(refs, split):
    apart = [(refs[2 * i], refs[2 * i + 1]) for i in range(split)]
    return apart + [(r, r) for r in refs[2 * split :]]


def base_kernel(count, rows, places, split, turn_ref, *refs):
    taken = count + split
    pieces = pair_up(refs[:taken], split)
    sound_ref, high_ref, low_ref = refs[taken : taken + 3]
    out_ref, flat_ref = refs[-2:]
    operate(pieces, rows, places, turn_ref, sound_ref, high_ref, low_ref, flat_ref, out_ref)


def add_terms(coefs, source_ref, source, flame_ref, image_ref):
    temp_re, temp_im, gain_re, gain_im = coefs
    for at in range(0, flame_ref.shape[1], LANES):
        cut = slice(at, at + LANES)
        flame = flame_ref[:, cut]
        base_re = source_ref[source, 0, :, cut]
        base_im = source_ref[source, 1, :, cut]
        field_re = source_ref[source, 2, :, cut]
        field_im = source_ref[source, 3, :, cut]
        image_ref[0, :, cut] += (
            temp_re * base_re - temp_im * base_im + flame * (gain_re * field_re - gain_im * field_im)
        )
        image_ref[1, :, cut] += (
            temp_re * base_im + temp_im * base_re + flame * (gain_re * field_im + gain_im * field_re)
        )


def inner_products(rows, coefs, source_ref, source, adjoint_ref, flame_ref, sums_ref, at_re, at_im):
    temp_re, temp_im, gain_re, gain_im = coefs

    def fold(x):
        out = x[0:8]
        for low in range(8, rows, 8):
            out = out + x[low : low + 8]
        return out

    sums = [jnp.zeros((8, LANES), jnp.float32)] * 4
    for at in range(0, flame_ref.shape[1], LANES):
        cut = slice(at, at + LANES)
        flame = flame_ref[:, cut]
        adj_re = adjoint_ref[0, :, cut]
        adj_im = adjoint_ref[1, :, cut]
        base_re = source_ref[source, 0, :, cut]
        base_im = source_ref[source, 1, :, cut]
        field_re = flame * source_ref[source, 2, :, cut]
        field_im = flame * source_ref[source, 3, :, cut]
        sums[0] = sums[0] + fold(adj_re * base_re + adj_im * base_im)
        sums[1] = sums[1] + fold(adj_re * base_im - adj_im * base_re)
        sums[2] = sums[2] + fold(adj_re * field_re + adj_im * field_im)
        sums[3] = sums[3] + fold(adj_re * field_im - adj_im * field_re)
    sums_ref[at_re] = temp_re * sums[0] - temp_im * sums[1] + gain_re * sums[2] - gain_im * sums[3]
    sums_ref[at_im] = temp_re * sums[1] + temp_im * sums[0] + gain_re * sums[3] + gain_im * sums[2]


def coefs_of(coef_ref, j):
    return tuple(coef_ref[8 * p + j : 8 * p + j + 1, :] for p in range(4))


def source_of(half, offsets_ref, t, j):
    own = lax.axis_index("order")
    orders = 2 * half
    place = (((own ^ t) - offsets_ref[j] + orders) & (orders - 1)) ^ own
    quarter = half // 2
    later = half + (place & (quarter - 1)) * 2 + ((place & quarter) // quarter)
    return jnp.where(place < half, place, later)


def cross_order(half):
    return [t + far for t in range(half // 2) for far in (0, half // 2)]


def early_kernel(half, count_offs, ready, offsets_ref, coef_ref, own_ref, cross_ref, flame_ref, image_ref):
    for t in range(half):
        image_ref[t, 0] = own_ref[t, 0]
        image_ref[t, 1] = own_ref[t, 1]
        for j in range(count_offs):
            source = source_of(half, offsets_ref, t, j)

            @pl.when(source < half)
            def _(t=t, j=j, source=source):
                add_terms(coefs_of(coef_ref, j), own_ref, source, flame_ref, image_ref.at[t])

            @pl.when((source >= half) & (source < ready))
            def _(t=t, j=j, source=source):
                add_terms(coefs_of(coef_ref, j), cross_ref, source - half, flame_ref, image_ref.at[t])


def late_kernel(half, rows, slabs, count_offs, ready, offsets_ref, coef_ref, turn_ref, *refs):
    count = 2 * half - ready
    pieces = pair_up(refs[:count], 0)
    sound_ref, high_ref, low_ref, flame_ref, image_in_ref, sums_in_ref = refs[count : count + 6]
    adjoint_refs = refs[count + 6 : count + 6 + half]
    image_refs = refs[count + 6 + half : count + 6 + 2 * half]
    out_ref, site_ref, flat_ref, sums_ref = refs[count + 6 + 2 * half :]
    here = lax.axis_index("order") % half
    places = [half + t for t in cross_order(half)[-count:]]
    operate(pieces, rows, places, turn_ref, sound_ref, high_ref, low_ref, flat_ref, site_ref)
    sums_ref[...] = sums_in_ref[...]
    for t in range(half):
        image_refs[t][...] = image_in_ref[t]
        for j in range(count_offs):
            source = source_of(half, offsets_ref, t, j)

            @pl.when(source >= ready)
            def _(t=t, j=j, source=source):
                coefs = coefs_of(coef_ref, j)
                add_terms(coefs, site_ref, source - ready, flame_ref, image_refs[t])
                inner_products(
                    rows, coefs, site_ref, source - ready, adjoint_refs[t], flame_ref, sums_ref,
                    t * 2 * count_offs + j, t * 2 * count_offs + count_offs + j,
                )

    for t in range(half):
        totals = [
            jnp.sum(sums_ref[t * 2 * count_offs + i], axis=0, keepdims=True)
            for i in range(2 * count_offs)
        ]
        totals = jnp.concatenate(totals, axis=0)
        for slab in range(slabs):
            place = pl.multiple_of(((here ^ t) * slabs + slab) * 8, 8)
            out_ref[pl.ds(place, 8), :] = totals


def couple_kernel(half, rows, count_offs, ready, partners, offsets_ref, coef_ref, own_ref, cross_ref, *refs):
    adjoint_refs = refs[: len(partners)]
    flame_ref, *before_refs, sums_ref = refs[len(partners) :]
    for before_ref in before_refs:
        sums_ref[...] = before_ref[...]
    for adjoint_ref, t in zip(adjoint_refs, partners):
        for j in range(count_offs):
            source = source_of(half, offsets_ref, t, j)

            def product(source_ref, place, adjoint_ref=adjoint_ref, t=t, j=j):
                inner_products(
                    rows, coefs_of(coef_ref, j), source_ref, place, adjoint_ref, flame_ref, sums_ref,
                    t * 2 * count_offs + j, t * 2 * count_offs + count_offs + j,
                )

            @pl.when(source < half)
            def _(product=product, source=source):
                product(own_ref, source)

            @pl.when((source >= half) & (source < ready))
            def _(product=product, source=source):
                product(cross_ref, source - half)


def place_kernel(half, rows, count_offs, scale, *refs):
    piece_refs, parts_ref = refs[:half], refs[half]
    image_ref, out_ref, coupling_ref, sems = refs[half + 1 :]
    here = lax.axis_index("order") % half
    copies = []
    for t in range(half):
        start = pl.multiple_of((here ^ t) * rows, rows)
        copies.append(pltpu.make_async_copy(piece_refs[t], image_ref.at[:, pl.ds(start, rows), :], sems.at[t]))
        copies[-1].start()
    total = jnp.sum(jnp.sum(parts_ref[...], axis=0), axis=1, keepdims=True) * scale
    total = jnp.broadcast_to(total, (8, count_offs))
    row = lax.broadcasted_iota(jnp.int32, (8, count_offs), 0)
    col = lax.broadcasted_iota(jnp.int32, (8, count_offs), 1)
    for part in range(2):
        picked = jnp.where(row == part * count_offs + col, total, 0.0)
        coupling_ref[0, part : part + 1, :] = jnp.sum(picked, axis=0, keepdims=True)
    copies.append(pltpu.make_async_copy(coupling_ref, out_ref, sems.at[half]))
    copies[-1].start()
    for copy in copies:
        copy.wait()


VMEM_SPEC = pl.BlockSpec(memory_space=VMEM)


def call(kernel, ins, spaces, outs, scratch=(), out_specs=None, limit=LIMIT):
    return pl.pallas_call(
        kernel,
        out_shape=outs,
        in_specs=[pl.BlockSpec(memory_space=s) for s in spaces],
        out_specs=jax.tree.map(lambda _: VMEM_SPEC, outs) if out_specs is None else out_specs,
        scratch_shapes=list(scratch),
        compiler_params=pltpu.CompilerParams(vmem_limit_bytes=limit),
    )(*ins)


def local(
    direct, adjoint, sound, transverse, burner_temp, burner_gain, flame_cells, flame_weight, offsets
):
    f32 = jnp.float32
    orders = lax.axis_size("order")
    slabs = lax.axis_size("slab")
    order_now = lax.axis_index("order")
    half = orders // 2
    layers, width = direct.shape[2:]
    mid = width // 2
    rows = layers // half
    count_offs = offsets.shape[0]
    here = order_now % half
    block_rows = 2 * (rows // 8) * 2 * 8 + 8
    ready = orders - LATE

    def of(*shape, dtype=f32):
        return jax.ShapeDtypeStruct(shape, dtype)

    def swap(value, t):
        return lax.ppermute(value, "order", [(i, i ^ t) for i in range(orders)])

    field = direct[0]
    arrivals = cross_order(half)
    bare = arrivals[:BARE]
    *bodies, top, bottom = call(
        functools.partial(first_kernel, half, rows, bare),
        (field, sound),
        (pltpu.HBM, pltpu.HBM),
        [of(2, rows, width)] * BARE + [of(8, mid), of(8, mid)],
        [pltpu.VMEM((2, 8, width), f32), pltpu.VMEM((8, width), f32)] * 2
        + [pltpu.SemaphoreType.DMA((4 + BARE,))],
        limit=None,
    )
    if slabs == 2:
        above = below = lax.ppermute(top, "slab", [(0, 1), (1, 0)])
    else:
        above = lax.ppermute(bottom, "slab", [(i, i + 1) for i in range(slabs - 1)])
        below = lax.ppermute(top, "slab", [(i + 1, i) for i in range(slabs - 1)])

    sent = call(
        functools.partial(pack_kernel, half, rows, bare),
        (field, above, below),
        (VMEM,) * 3,
        [of(block_rows, mid)] * half + [of(8, mid)] * BARE,
    )
    halos = sent[half:]
    sound_site = call(
        functools.partial(sound_kernel, half, rows), (sound, above, below), (VMEM,) * 3, of(rows + 8, width)
    )
    own = [sent[0]] + [swap(sent[t], t) for t in range(1, half)]
    pieces = []
    for t, body, halo in zip(bare, bodies, halos):
        pieces += [swap(body, half ^ t), swap(halo, half ^ t)]
    cross = [swap(sent[t], half ^ t) for t in arrivals[BARE:]]
    pieces += cross[: half - BARE - LATE]

    adjoint_cut = adjoint[0].reshape(2, half, rows, width)
    adj_sent = [lax.dynamic_index_in_dim(adjoint_cut, here ^ t, 1, keepdims=False) for t in range(half)]
    adj = [adj_sent[0]] + [swap(adj_sent[t], t) for t in range(1, half)]

    high, low = call(split_kernel, (transverse,), (VMEM,), [of(*transverse.shape, dtype=jnp.bfloat16)] * 2)
    turn, coef = call(
        functools.partial(table_kernel, orders),
        (offsets, burner_temp.reshape(1, -1), burner_gain.reshape(1, -1)),
        (SMEM, VMEM, VMEM),
        [of(2 * orders, LANES), of(32, LANES)],
    )
    flame = call(
        functools.partial(flame_kernel, half, rows, 4),
        (flame_cells.reshape(-1, LANES), flame_weight.reshape(-1, LANES)),
        (VMEM, VMEM),
        of(rows, width),
    )

    def base(pieces, places, split):
        return call(
            functools.partial(base_kernel, len(places), rows, places, split),
            (turn, *pieces, sound_site, high, low),
            (VMEM,) * (len(pieces) + 4),
            of(len(places), 4, rows, width),
            [pltpu.VMEM((len(places) * 2 * rows, width), f32)],
        )

    site_own = base(own, list(range(half)), 0)
    site_cross = base(pieces, [half + t for t in arrivals[:-LATE]], BARE)
    image_early = call(
        functools.partial(early_kernel, half, count_offs, ready),
        (offsets, coef, site_own, site_cross, flame),
        (SMEM,) + (VMEM,) * 4,
        of(half, 2, rows, width),
    )
    sums_shape = (half * 2 * count_offs, 8, LANES)
    sums_early = ()
    partners = [0] + sorted(even_first(half), key=lambda t: t & 1 and t >= half // 2)
    for some in (partners[:-LAST], partners[-LAST:]):
        sums_early = call(
            functools.partial(couple_kernel, half, rows, count_offs, ready, some),
            (offsets, coef, site_own, site_cross, *(adj[t] for t in some), flame, *sums_early),
            (SMEM,) + (VMEM,) * (len(some) + 4 + len(sums_early)),
            [of(*sums_shape)],
        )
    *images, sums = call(
        functools.partial(late_kernel, half, rows, slabs, count_offs, ready),
        (offsets, coef, turn, *cross[half - BARE - LATE :], sound_site, high, low, flame, image_early, *sums_early, *adj),
        (SMEM,) + (VMEM,) * (LATE + half + 8),
        [of(2, rows, width)] * half + [of(half * slabs * 8, LANES)],
        [
            pltpu.VMEM((LATE, 4, rows, width), f32),
            pltpu.VMEM((LATE * 2 * rows, width), f32),
            pltpu.VMEM(sums_shape, f32),
        ],
    )

    back = [images[0]] + [swap(images[t], t) for t in range(1, half)]
    groups = [list(range(half * slabs)), list(range(half * slabs, orders * slabs))]
    parts = lax.all_to_all(
        sums.reshape(half * slabs, 8, LANES), ("order", "slab"), 0, 0, axis_index_groups=groups, tiled=True
    )
    scale = 1.0 / math.sqrt(layers * slabs * width)
    image, coupling = call(
        functools.partial(place_kernel, half, rows, count_offs, scale),
        (*back, parts),
        (VMEM,) * (half + 1),
        [of(2, layers, width), of(1, 2, count_offs)],
        [pltpu.VMEM((1, 2, count_offs), f32), pltpu.SemaphoreType.DMA((half + 1,))],
        [pl.BlockSpec(memory_space=pltpu.HBM)] * 2,
    )
    return (image[None], coupling)


def even_first(half):
    return sorted(range(1, half), key=lambda t: (t & 1, -t))


def solution(mesh):
    in_specs = (
        P("order", None, "slab", None),
        P("order", None, "slab", None),
        P("slab", None),
        P(),
        P(),
        P(),
        P(),
        P(),
        P(),
    )
    out_specs = (P("order", None, "slab", None), P("order", None, None))

    return jax.shard_map(local, mesh=mesh, in_specs=in_specs, out_specs=out_specs, check_vma=False)
```
